32 devices in a mesh: groups: 2 (over x), lat: 16 (over z, y, core).
Axes of the slice: x: 2, y: 2, z: 4, core: 2. Of those that a mesh axis runs over, the one named last changes fastest.
Arguments:
- objects: float32 [2, 2, 8192, 1024], P(None, None, ('groups', 'lat')), parts along dimension 2, may hold values from -5 to 5
- probes: float32 [4, 2, 256, 256], P('groups'), parts along dimension 0, may hold values from -5 to 5
- x_offsets: int32 [64], P(('groups', 'lat')), parts along dimension 0, may hold values from 0 to 255
- y_offsets: int32 [64], P(('groups', 'lat')), parts along dimension 0, may hold values from 0 to 768
- modes: int32 [64], P(('groups', 'lat')), parts along dimension 0, may hold values from 0 to 1
- measured: float32 [64, 256, 256], P(('groups', 'lat')), parts along dimension 0, may hold values from 0 to 2
Outputs:
- updated: float32 [2, 2, 8192, 1024], P(None, None, ('groups', 'lat')), parts along dimension 2
The draws below stay inside these ranges and needn't reach their ends.
There are 2 independent parts, one for each index of `groups`. The reference program is written for one: setup_inputs(seed, part) draws one part's arguments, and reference() takes and returns one part's arrays. A program takes and returns all parts, laid end to end along the dimension named above; each array names one. Nothing has to cross between parts.
All inputs are finite; a program needn't handle non-finite values.
Results may differ from the reference program's by a relative error of at most 0.0003.
Values sent between devices are 32-bit elements; how exact they have to be, the bound alone decides.
No kernel may reach another device: no remote copies, remote signals or barrier semaphores. Data moves between devices by JAX's collectives and lax.ppermute only.
A program may use at most 128 MiB of HBM per device.

```python
import jax
import jax.numpy as jnp
from jax import lax

W = 256
TILE = 256
OY = 1024
POS_DEV = 2
SLICES = 2
NPROBE = 2
NX = 4096
NPOS = 32
N_LAT = 16


def touch_ends(values, own_key, low, top_value):
    longest = values.shape.index(max(values.shape))
    spots = []
    for shift in (0, 1):
        where = [jax.random.randint(jax.random.fold_in(own_key, axis), (), 0, length) for axis, length in enumerate(values.shape)]
        where[longest] = (where[longest] + shift) % values.shape[longest]
        spots.append(tuple(where))
    return values.at[spots[0]].set(low).at[spots[1]].set(top_value)


def shard_levels(rng, dims, split, smallest, high):
    loudness = 1.0
    for dim, shards_of in split:
        heights = jax.random.uniform(jax.random.fold_in(jax.random.fold_in(rng, 6), dim), (shards_of,), jnp.float32, smallest / len(split), high / len(split))
        loudness = loudness * jnp.repeat(jnp.exp(heights), dims[dim] // shards_of).reshape((-1,) + (1,) * (len(dims) - 1 - dim))
    return loudness


def noise(own_key, dims, deviation, reach, shards=(), held_as=jnp.bfloat16):
    level = shard_levels(own_key, dims, shards, -0.22, 0.18) if shards else 1.0
    array = jax.random.normal(own_key, dims, jnp.float32) * deviation * level
    return jnp.minimum(jnp.maximum(array, -reach), reach).astype(held_as)


def setup_inputs(seed: int = 0, part: int = 0) -> dict:
    seeds = jax.random.split(jax.random.key(seed), 7)
    part_keys = jax.random.split(jax.random.fold_in(seeds[6], part), 7)
    objects = noise(part_keys[0], (SLICES, 2, NX, OY), 0.7, 5.0, ((2, 16),), jnp.float32)
    probes = noise(part_keys[1], (NPROBE, 2, W, W), 0.7, 5.0, (), jnp.float32)
    x_offsets = touch_ends(jax.random.randint(part_keys[2], (NPOS,), 0, TILE), jax.random.fold_in(part_keys[2], 1), 0, TILE - 1).astype(jnp.int32)
    y_offsets = touch_ends(jax.random.randint(part_keys[3], (NPOS,), 0, OY - W + 1), jax.random.fold_in(part_keys[3], 1), 0, OY - W).astype(jnp.int32)
    modes = touch_ends(jax.random.randint(part_keys[4], (NPOS,), 0, NPROBE), jax.random.fold_in(part_keys[4], 1), 0, NPROBE - 1).astype(jnp.int32)
    measured = jnp.clip(2.0 * jax.random.uniform(part_keys[5], (NPOS, W, W), jnp.float32) ** shard_levels(part_keys[5], (NPOS, W, W), ((0, 16),), -0.2, 0.2), 0.0, 2.0)
    return dict(objects=objects, probes=probes, x_offsets=x_offsets, y_offsets=y_offsets, modes=modes, measured=measured)


spread_phase = 40.0
descent_rate = 1.0


def kernel_phase(width):
    counter = jnp.arange(width, dtype=jnp.int32)
    folded = ((counter + width // 2) % width - width // 2).astype(jnp.float32) / width
    return spread_phase * (folded[:, None] ** 2 + folded[None, :] ** 2)


def propagate(wavefield, kernel):
    return jnp.fft.ifft2(jnp.fft.fft2(wavefield, norm="ortho") * kernel, norm="ortho")


def reference(objects, probes, x_offsets, y_offsets, modes, measured):
    transmission = objects[:, 0] + 1j * objects[:, 1]
    padded = jnp.concatenate([transmission, jnp.zeros_like(transmission[:, :TILE])], axis=1)
    probe_field = probes[:, 0] + 1j * probes[:, 1]
    forward_kernel = jnp.exp(-1j * kernel_phase(W))
    anchor = jnp.zeros((), jnp.int32)
    positions = jnp.arange(POS_DEV * N_LAT, dtype=jnp.int32)

    def visit(gradient, record):
        position, x_offset, y_offset, probe_mode, intensity = record
        corner = (anchor, (position // POS_DEV) * TILE + x_offset, y_offset)
        window = lax.dynamic_slice(padded, corner, (SLICES, W, W))
        wavefield = probe_field[probe_mode]
        entering = []
        for s in range(SLICES):
            if s > 0:
                wavefield = propagate(wavefield, forward_kernel)
            entering.append(wavefield)
            wavefield = wavefield * window[s]
        detector = jnp.fft.fft2(wavefield, norm="ortho")
        residual = detector.real ** 2 + detector.imag ** 2 - intensity
        adjoint = jnp.fft.ifft2(residual * detector, norm="ortho")
        pieces = [None] * SLICES
        for s in reversed(range(SLICES)):
            pieces[s] = jnp.conj(entering[s]) * adjoint
            adjoint = jnp.conj(window[s]) * adjoint
            if s > 0:
                adjoint = propagate(adjoint, jnp.conj(forward_kernel))
        current = lax.dynamic_slice(gradient, corner, (SLICES, W, W))
        return lax.dynamic_update_slice(gradient, current + jnp.stack(pieces), corner), None

    gradient, _ = lax.scan(visit, jnp.zeros_like(padded), (positions, x_offsets, y_offsets, modes, measured))
    gradient = gradient[:, :NX]
    updated = transmission - descent_rate * gradient
    return jnp.stack([updated.real, updated.imag], axis=1).astype(jnp.float32)
```

```python
import functools
import math

import jax
import jax.numpy as jnp
import numpy as np
from jax import lax
from jax.experimental import pallas as pl
from jax.experimental.pallas import tpu as pltpu
from jax.sharding import PartitionSpec as P

SPREAD_PHASE = 40.0
LANES = 128


def permute_along(block, axis, distance):
    devices = range(lax.axis_size(axis))
    route = [(i - distance, i) for i in devices if i - distance in devices]
    return lax.ppermute(block, axis, route)


def matrix_tables(width):
    counter = np.arange(width)
    angles = (counter[:, None] * counter[None, :] % width) * (2.0 * math.pi / width)
    wave = np.exp(1j * angles) / math.sqrt(width)
    folded = ((counter + width // 2) % width - width // 2) / width
    phases = np.exp(-1j * SPREAD_PHASE * folded**2)
    spread = (wave * phases[None, :]) @ np.conj(wave)
    spread = (spread + spread.T) / 2
    stacked = np.stack([spread.real, spread.imag, wave.real, wave.imag])
    high = stacked.astype(jnp.bfloat16)
    low = (stacked - high.astype(np.float64)).astype(jnp.bfloat16)
    return high, low


def split(value):
    high = value.astype(jnp.bfloat16)
    return high, (value - high.astype(jnp.float32)).astype(jnp.bfloat16)


def pack_kernel(scalars, a_ref, b_ref, c_ref, out_ref):
    shift = scalars[1]
    wide = jnp.concatenate([a_ref[0, 0], b_ref[0, 0], c_ref[0, 0]], axis=1)
    width = wide.shape[1]
    out_ref[0, 0] = pltpu.roll(wide, width - shift, 1)[:, : out_ref.shape[3]]


def pack_windows(objects, columns, window):
    slices, parts, tile, _ = objects.shape

    def block(j):
        return pl.BlockSpec(
            (1, 1, tile, LANES), lambda i, s: (i // parts, i % parts, 0, s[0] + j)
        )

    return pl.pallas_call(
        pack_kernel,
        grid_spec=pltpu.PrefetchScalarGridSpec(
            num_scalar_prefetch=1,
            grid=(slices * parts,),
            in_specs=[block(0), block(1), block(2)],
            out_specs=pl.BlockSpec((1, 1, tile, window), lambda i, s: (i // parts, i % parts, 0, 0)),
        ),
        out_shape=jax.ShapeDtypeStruct((slices, parts, tile, window), jnp.float32),
        cost_estimate=pl.CostEstimate(flops=10**6, bytes_accessed=10 * 2**18, transcendentals=0),
        name="pack",
    )(columns, objects, objects, objects)


def cmul(ar, ai, br, bi):
    return ar * br - ai * bi, ar * bi + ai * br


def cmul_conj(ar, ai, br, bi):
    return ar * br + ai * bi, ar * bi - ai * br


def window_kernel(scalars, a_ref, b_ref, c_ref, recv_ref, probe_ref, measured_ref,
                  col_high, col_low, row_high, row_low, own_ref, ret_ref,
                  extended, win, left_high, left_low, right_high, right_low, entry, field):
    shift, rows = scalars[1], scalars[2]
    slices, parts, tile, window = recv_ref.shape
    offset = lax.rem(rows, 8)
    base = pl.multiple_of(rows - offset, 8)
    padded = window + 8

    for s in range(slices):
        for c in range(parts):
            wide = jnp.concatenate([a_ref[s, c], b_ref[s, c], c_ref[s, c]], axis=1)
            extended[0:tile] = pltpu.roll(wide, wide.shape[1] - shift, 1)[:, :window]
            extended[tile : 2 * tile] = recv_ref[s, c]
            loaded = extended[pl.ds(base, padded), :]
            win[s, c] = pltpu.roll(loaded, padded - offset, 0)[:window]

    def transform(real, imag, table, sign):
        high, low = split(real)
        left_high[0:window, 0:window] = high
        left_low[0:window, 0:window] = low
        left_high[window:, window:] = high * sign
        left_low[window:, window:] = low * sign
        high, low = split(imag)
        left_high[window:, 0:window] = high
        left_low[window:, 0:window] = low
        left_high[0:window, window:] = high * -sign
        left_low[0:window, window:] = low * -sign
        product = functools.partial(jnp.dot, preferred_element_type=jnp.float32)
        last = (product(left_high[...], col_high[table]) + product(left_high[...], col_low[table])
                + product(left_low[...], col_high[table]))
        high, low = split(last[0:window])
        right_high[0:window, 0:window] = high
        right_low[0:window, 0:window] = low
        right_high[window:, window:] = high * sign
        right_low[window:, window:] = low * sign
        high, low = split(last[window:])
        right_high[0:window, window:] = high
        right_low[0:window, window:] = low
        right_high[window:, 0:window] = high * -sign
        right_low[window:, 0:window] = low * -sign
        first = (product(row_high[table], right_high[...]) + product(row_high[table], right_low[...])
                 + product(row_low[table], right_high[...]))
        return first[:, 0:window], first[:, window:]

    def store_piece(s, piece):
        for c in range(parts):
            value = jnp.concatenate([piece[c], jnp.zeros((8, window), jnp.float32)], axis=0)
            extended[...] = jnp.zeros_like(extended)
            extended[pl.ds(base, padded), :] = pltpu.roll(value, offset, 0)
            own_ref[s, c] = extended[0:tile]
            ret_ref[s, c] = extended[tile : 2 * tile]

    one = jnp.bfloat16(1)
    er, ei = transform(*cmul(probe_ref[0, 0], probe_ref[0, 1], win[0, 0], win[0, 1]), 0, one)
    entry[0] = er
    entry[1] = ei
    fr, fi = transform(*cmul(entry[0], entry[1], win[1, 0], win[1, 1]), 1, -one)
    residual = fr * fr + fi * fi - measured_ref[0]
    gr, gi = transform(residual * fr, residual * fi, 1, one)
    field[0] = gr
    field[1] = gi
    store_piece(1, cmul_conj(entry[0], entry[1], field[0], field[1]))
    gr, gi = transform(*cmul_conj(win[1, 0], win[1, 1], field[0], field[1]), 0, -one)
    field[0] = gr
    field[1] = gi
    store_piece(0, cmul_conj(probe_ref[0, 0], probe_ref[0, 1], field[0], field[1]))


def window_gradient(objects, received, probes, measured, tables, scalars, position):
    slices, parts, tile, _ = objects.shape
    window = measured.shape[-1]
    shape = (slices, parts, tile, window)

    def block(j):
        return pl.BlockSpec((slices, parts, tile, LANES), lambda i, s: (0, 0, 0, s[0] + j))

    def whole(array):
        return pl.BlockSpec(array.shape, lambda i, s: (0,) * array.ndim)

    return pl.pallas_call(
        window_kernel,
        grid_spec=pltpu.PrefetchScalarGridSpec(
            num_scalar_prefetch=1,
            grid=(1,),
            in_specs=[
                block(0), block(1), block(2),
                whole(received),
                pl.BlockSpec((1, parts, window, window), lambda i, s: (s[3], 0, 0, 0)),
                pl.BlockSpec((1, window, window), lambda i, s: (position, 0, 0)),
                *[whole(t) for t in tables],
            ],
            out_specs=[pl.BlockSpec(shape, lambda i, s: (0, 0, 0, 0))] * 2,
            scratch_shapes=[
                pltpu.VMEM((2 * tile + 8, window), jnp.float32),
                pltpu.VMEM((slices, parts, window, window), jnp.float32),
                *[pltpu.VMEM((2 * window, 2 * window), jnp.bfloat16)] * 4,
                pltpu.VMEM((parts, window, window), jnp.float32),
                pltpu.VMEM((parts, window, window), jnp.float32),
            ],
        ),
        out_shape=[jax.ShapeDtypeStruct(shape, jnp.float32)] * 2,
        cost_estimate=pl.CostEstimate(flops=6 * 10**9, bytes_accessed=6 * 2**20, transcendentals=0),
        name="window_gradient",
    )(scalars, objects, objects, objects, received, probes, measured, *tables)


def final_kernel(scalars, objects_ref, *refs):
    piece_refs, out_ref = refs[:-1], refs[-1]
    out_ref[...] = objects_ref[...]
    for k, piece_ref in enumerate(piece_refs):
        start = pl.multiple_of(scalars[2 * k] * LANES, LANES)
        piece = piece_ref[0, 0]
        wide = jnp.concatenate([piece, jnp.zeros((piece.shape[0], LANES), jnp.float32)], axis=1)
        columns = pl.ds(start, wide.shape[1])
        out_ref[0, 0, :, columns] = out_ref[0, 0, :, columns] - pltpu.roll(wide, scalars[2 * k + 1], 1)


def subtract_pieces(objects, pieces, columns):
    slices, parts, tile, length = objects.shape
    index = lambda i, s: (i // parts, i % parts, 0, 0)
    return pl.pallas_call(
        final_kernel,
        grid_spec=pltpu.PrefetchScalarGridSpec(
            num_scalar_prefetch=1,
            grid=(slices * parts,),
            in_specs=[pl.BlockSpec((1, 1, tile, length), index)]
            + [pl.BlockSpec((1, 1) + piece.shape[2:], index) for piece in pieces],
            out_specs=pl.BlockSpec((1, 1, tile, length), index),
        ),
        out_shape=jax.ShapeDtypeStruct(objects.shape, jnp.float32),
        cost_estimate=pl.CostEstimate(flops=10**6, bytes_accessed=12 * 2**20, transcendentals=0),
        name="subtract",
    )(columns, objects, *pieces)


def on_device(objects, probes, x_offsets, y_offsets, modes, measured):
    amount, window = measured.shape[0], measured.shape[-1]
    length = objects.shape[-1]
    high, low = matrix_tables(window)
    columns = lambda t: jnp.asarray(np.concatenate([t[0::2], t[1::2]], axis=1))
    rows = lambda t: jnp.asarray(np.concatenate([t[0::2], t[1::2]], axis=2))
    tables = (columns(high), columns(low), rows(high), rows(low))

    def blocks_of(offsets):
        block = jnp.minimum(offsets // LANES, (length - window) // LANES - 1)
        return jnp.stack([block, offsets - block * LANES], axis=1)

    left_blocks = blocks_of(permute_along(y_offsets, "lat", 1))
    own_blocks = blocks_of(y_offsets)
    sent = [pack_windows(objects, left_blocks[p], window) for p in range(amount)]
    received = [permute_along(block, "lat", -1) for block in sent]
    own, returned = [], []
    for p in range(amount):
        scalars = jnp.concatenate([own_blocks[p], x_offsets[p : p + 1], modes[p : p + 1]])
        mine, theirs = window_gradient(objects, received[p], probes, measured, tables, scalars, p)
        own.append(mine)
        returned.append(permute_along(theirs, "lat", 1))
    where = jnp.concatenate([own_blocks.reshape(-1), left_blocks.reshape(-1)])
    return subtract_pieces(objects, own + returned, where)


def solution(mesh):
    in_specs = (
        P(None, None, ("groups", "lat"), None),
        P("groups", None, None, None),
        P(("groups", "lat")),
        P(("groups", "lat")),
        P(("groups", "lat")),
        P(("groups", "lat"), None, None),
    )
    out_specs = P(None, None, ("groups", "lat"), None)
    return jax.shard_map(
        on_device, mesh=mesh, in_specs=in_specs, out_specs=out_specs, check_vma=False
    )
```

```python
import functools
import math

import jax
import jax.numpy as jnp
import numpy as np
from jax import lax
from jax.experimental import pallas as pl
from jax.experimental.pallas import tpu as pltpu
from jax.sharding import PartitionSpec as P

SPREAD_PHASE = 40.0
LANES = 128


def permute_along(block, axis, distance):
    devices = range(lax.axis_size(axis))
    route = [(i - distance, i) for i in devices if i - distance in devices]
    return lax.ppermute(block, axis, route)


def matrix_tables(width):
    counter = np.arange(width)
    angles = (counter[:, None] * counter[None, :] % width) * (2.0 * math.pi / width)
    wave = np.exp(-1j * angles) / math.sqrt(width)
    folded = ((counter + width // 2) % width - width // 2) / width
    phases = np.exp(-1j * SPREAD_PHASE * folded**2)
    spread = (np.conj(wave) * phases[None, :]) @ wave
    spread = (spread + spread.T) / 2
    stacked = np.stack([np.block([[t.real, t.imag], [-t.imag, t.real]]) for t in (spread, wave)])
    high = stacked.astype(jnp.bfloat16)
    low = (stacked - high.astype(np.float64)).astype(jnp.bfloat16)
    return jnp.asarray(high), jnp.asarray(low)


def split(value):
    high = value.astype(jnp.bfloat16)
    return high, (value - high.astype(jnp.float32)).astype(jnp.bfloat16)


VMEM = pl.BlockSpec(memory_space=pltpu.VMEM)
PARAMS = pltpu.CompilerParams(vmem_limit_bytes=24 * 2**20)


def on_chip(array):
    return pltpu.with_memory_space_constraint(array, pltpu.VMEM)


SMEM = pl.BlockSpec(memory_space=pltpu.SMEM)


def column_block(offset, window, length):
    block = jnp.minimum(offset // LANES, (length - window) // LANES - 1)
    return block, offset - block * LANES


def columns_at(tile_ref, s, c, rows, offset, window):
    block, shift = column_block(offset, window, tile_ref.shape[-1])
    lane = lax.broadcasted_iota(jnp.int32, (rows.size, LANES), 1)
    turned = []
    for j in range(window // LANES + 1):
        start = pl.multiple_of((block + j) * LANES, LANES)
        turned.append(pltpu.roll(tile_ref[s, c, rows, pl.ds(start, LANES)], LANES - shift, 1))
    return [jnp.where(lane < LANES - shift, turned[j], turned[j + 1]) for j in range(window // LANES)]


def subtract_at(tile_ref, s, c, rows, offset, piece):
    window = piece.shape[1]
    block, shift = column_block(offset, window, tile_ref.shape[-1])
    lane = lax.broadcasted_iota(jnp.int32, (rows.size, LANES), 1)
    parts = window // LANES
    turned = [pltpu.roll(piece[:, j * LANES : (j + 1) * LANES], shift, 1) for j in range(parts)]
    for j in range(parts + 1):
        start = pl.multiple_of((block + j) * LANES, LANES)
        above = turned[j - 1] if j > 0 else jnp.zeros_like(turned[0])
        here = turned[j] if j < parts else jnp.zeros_like(turned[0])
        columns = pl.ds(start, LANES)
        tile_ref[s, c, rows, columns] = tile_ref[s, c, rows, columns] - jnp.where(lane < shift, above, here)


def planes(ref):
    return [(s, c) for s in range(ref.shape[0]) for c in range(ref.shape[1])]


def pack_kernel(position, offsets, tile_ref, out_ref):
    _, _, tile, window = out_ref.shape
    for s, c in planes(out_ref):
        parts = columns_at(tile_ref, s, c, pl.ds(0, tile), offsets[position], window)
        for j, part in enumerate(parts):
            out_ref[s, c, :, j * LANES : (j + 1) * LANES] = part


def pack_windows(objects, offsets, position, window):
    shape = objects.shape[:3] + (window,)
    return pl.pallas_call(
        functools.partial(pack_kernel, position),
        in_specs=[SMEM, VMEM],
        out_specs=VMEM,
        out_shape=pltpu.VMEM(shape, jnp.float32),
        compiler_params=PARAMS,
        cost_estimate=pl.CostEstimate(flops=10**6, bytes_accessed=2**21, transcendentals=0),
        name="pack",
    )(offsets, objects)


def cmul(ar, ai, br, bi):
    return ar * br - ai * bi, ar * bi + ai * br


def cmul_conj(ar, ai, br, bi):
    return ar * br + ai * bi, ar * bi - ai * br


def window_kernel(position, x_offsets, y_offsets, modes, tile_ref, recv_ref, probe_ref, measured_ref,
                  high_ref, low_ref, state_ref, total_ref, ret_ref,
                  extended, win, left_high, left_low, right_high, right_low, entry, field):
    slices, parts, tile, window = recv_ref.shape
    x_offset, y_offset, mode = x_offsets[position], y_offsets[position], modes[position]
    offset = lax.rem(x_offset, 8)
    base = pl.multiple_of(x_offset - offset, 8)
    padded = window + 8

    for s, c in planes(recv_ref):
        for j, part in enumerate(columns_at(tile_ref, s, c, pl.ds(0, tile), y_offset, window)):
            extended[0:tile, j * LANES : (j + 1) * LANES] = part
        extended[tile : 2 * tile] = recv_ref[s, c]
        loaded = extended[pl.ds(base, padded), :]
        win[s, c] = pltpu.roll(loaded, padded - offset, 0)[:window]

    product = functools.partial(jnp.dot, preferred_element_type=jnp.float32)

    def transform(real, imag, table):
        left_high[:, 0:window], left_low[:, 0:window] = split(real)
        left_high[:, window:], left_low[:, window:] = split(imag)
        last = (product(left_high[...], high_ref[table]) + product(left_high[...], low_ref[table])
                + product(left_low[...], high_ref[table]))
        high, low = split(last[:, 0:window])
        right_high[0:window, 0:window] = high
        right_low[0:window, 0:window] = low
        right_high[window:, window:] = high
        right_low[window:, window:] = low
        high, low = split(last[:, window:])
        right_high[0:window, window:] = high
        right_low[0:window, window:] = low
        right_high[window:, 0:window] = -high
        right_low[window:, 0:window] = -low
        high, low = high_ref[table, 0:window], low_ref[table, 0:window]
        first = (product(high, right_high[...]) + product(high, right_low[...])
                 + product(low, right_high[...]))
        return first[:, 0:window], first[:, window:]

    def transform_conj(real, imag, table):
        real, imag = transform(real, -imag, table)
        return real, -imag

    def store_piece(s, piece):
        for c in range(parts):
            value = jnp.concatenate([piece[c], jnp.zeros((8, window), jnp.float32)], axis=0)
            extended[...] = jnp.zeros_like(extended)
            extended[pl.ds(base, padded), :] = pltpu.roll(value, offset, 0)
            ret_ref[s, c] = extended[tile : 2 * tile]
            subtract_at(total_ref, s, c, pl.ds(0, tile), y_offset, extended[0:tile])

    entry[0], entry[1] = transform(*cmul(probe_ref[mode, 0], probe_ref[mode, 1], win[0, 0], win[0, 1]), 0)
    fr, fi = transform(*cmul(entry[0], entry[1], win[1, 0], win[1, 1]), 1)
    residual = fr * fr + fi * fi - measured_ref[position]
    field[0], field[1] = transform_conj(residual * fr, residual * fi, 1)
    if position == 0:
        total_ref[...] = state_ref[...]
    store_piece(1, cmul_conj(entry[0], entry[1], field[0], field[1]))
    field[0], field[1] = transform_conj(*cmul_conj(win[1, 0], win[1, 1], field[0], field[1]), 0)
    store_piece(0, cmul_conj(probe_ref[mode, 0], probe_ref[mode, 1], field[0], field[1]))


def window_gradient(objects, total, received, probes, measured, tables, offsets, position):
    window = measured.shape[-1]
    parts = objects.shape[1]
    return pl.pallas_call(
        functools.partial(window_kernel, position),
        in_specs=[SMEM] * 3 + [VMEM] * 7,
        out_specs=[VMEM, VMEM],
        scratch_shapes=[
            pltpu.VMEM((objects.shape[2] + window + 8, window), jnp.float32),
            pltpu.VMEM(received.shape, jnp.float32),
            *[pltpu.VMEM((window, 2 * window), jnp.bfloat16)] * 2,
            *[pltpu.VMEM((2 * window, 2 * window), jnp.bfloat16)] * 2,
            pltpu.VMEM((parts, window, window), jnp.float32),
            pltpu.VMEM((parts, window, window), jnp.float32),
        ],
        out_shape=[pltpu.VMEM(objects.shape, jnp.float32), pltpu.VMEM(received.shape, jnp.float32)],
        compiler_params=PARAMS,
        input_output_aliases={9: 0} if position else {},
        cost_estimate=pl.CostEstimate(flops=6 * 10**9, bytes_accessed=6 * 2**20, transcendentals=0),
        name="window_gradient",
    )(*offsets, objects, received, probes, measured, *tables, total)


def subtract_kernel(position, offsets, piece_ref, state_ref, out_ref):
    del state_ref
    for s, c in planes(piece_ref):
        subtract_at(out_ref, s, c, pl.ds(0, piece_ref.shape[2]), offsets[position], piece_ref[s, c])


def subtract_window(total, piece, offsets, position):
    return pl.pallas_call(
        functools.partial(subtract_kernel, position),
        in_specs=[SMEM, VMEM, VMEM],
        out_specs=VMEM,
        out_shape=pltpu.VMEM(total.shape, jnp.float32),
        compiler_params=PARAMS,
        input_output_aliases={2: 0},
        cost_estimate=pl.CostEstimate(flops=10**6, bytes_accessed=2**21, transcendentals=0),
        name="subtract",
    )(offsets, piece, total)


def on_device(objects, probes, x_offsets, y_offsets, modes, measured):
    amount, window = measured.shape[0], measured.shape[-1]
    tables = [on_chip(t) for t in matrix_tables(window)]
    objects, probes, measured = on_chip(objects), on_chip(probes), on_chip(measured)
    left_offsets = permute_along(y_offsets, "lat", 1)
    received = [
        on_chip(permute_along(pack_windows(objects, left_offsets, p, window), "lat", -1))
        for p in range(amount)
    ]
    total, returned = objects, []
    for p in range(amount):
        total, piece = window_gradient(
            objects, total, received[p], probes, measured, tables, (x_offsets, y_offsets, modes), p)
        returned.append(on_chip(permute_along(piece, "lat", 1)))
    for p in range(amount):
        total = subtract_window(total, returned[p], left_offsets, p)
    return total


def solution(mesh):
    in_specs = (
        P(None, None, ("groups", "lat"), None),
        P("groups", None, None, None),
        P(("groups", "lat")),
        P(("groups", "lat")),
        P(("groups", "lat")),
        P(("groups", "lat"), None, None),
    )
    out_specs = P(None, None, ("groups", "lat"), None)
    return jax.shard_map(
        on_device, mesh=mesh, in_specs=in_specs, out_specs=out_specs, check_vma=False
    )
```

```python
import functools
import math

import jax
import jax.numpy as jnp
import numpy as np
from jax import lax
from jax.experimental import pallas as pl
from jax.experimental.pallas import tpu as pltpu
from jax.sharding import PartitionSpec as P

SPREAD_PHASE = 40.0
LANES = 128


def permute_pairs(block, axis, pairs):
    return lax.ppermute(block, axis, pairs)


def route(axis, distance, keep=lambda i: True):
    devices = range(lax.axis_size(axis))
    return [(i, i + distance) for i in devices if i + distance in devices and keep(i)]


def matrix_tables(width):
    counter = np.arange(width)
    angles = (counter[:, None] * counter[None, :] % width) * (2.0 * math.pi / width)
    wave = np.exp(-1j * angles) / math.sqrt(width)
    folded = ((counter + width // 2) % width - width // 2) / width
    phases = np.exp(-1j * SPREAD_PHASE * folded**2)
    spread = (np.conj(wave) * phases[None, :]) @ wave
    spread = (spread + spread.T) / 2
    stacked = np.stack([np.block([[t.real, t.imag], [-t.imag, t.real]]) for t in (spread, wave)])
    high = stacked.astype(jnp.bfloat16)
    low = (stacked - high.astype(np.float64)).astype(jnp.bfloat16)
    return jnp.asarray(high), jnp.asarray(low)


def split(value):
    high = value.astype(jnp.bfloat16)
    return high, (value - high.astype(jnp.float32)).astype(jnp.bfloat16)


VMEM = pl.BlockSpec(memory_space=pltpu.VMEM)
PARAMS = pltpu.CompilerParams(vmem_limit_bytes=24 * 2**20)


def on_chip(array):
    return pltpu.with_memory_space_constraint(array, pltpu.VMEM)


SMEM = pl.BlockSpec(memory_space=pltpu.SMEM)


def column_block(offset, window, length):
    block = jnp.minimum(offset // LANES, (length - window) // LANES - 1)
    return block, offset - block * LANES


def columns_at(tile_ref, s, c, rows, offset, window):
    block, shift = column_block(offset, window, tile_ref.shape[-1])
    lane = lax.broadcasted_iota(jnp.int32, (rows.size, LANES), 1)
    turned = []
    for j in range(window // LANES + 1):
        start = pl.multiple_of((block + j) * LANES, LANES)
        turned.append(pltpu.roll(tile_ref[s, c, rows, pl.ds(start, LANES)], LANES - shift, 1))
    return [jnp.where(lane < LANES - shift, turned[j], turned[j + 1]) for j in range(window // LANES)]


def subtract_at(tile_ref, s, c, rows, offset, piece):
    window = piece.shape[1]
    block, shift = column_block(offset, window, tile_ref.shape[-1])
    lane = lax.broadcasted_iota(jnp.int32, (rows.size, LANES), 1)
    parts = window // LANES
    turned = [pltpu.roll(piece[:, j * LANES : (j + 1) * LANES], shift, 1) for j in range(parts)]
    for j in range(parts + 1):
        start = pl.multiple_of((block + j) * LANES, LANES)
        above = turned[j - 1] if j > 0 else jnp.zeros_like(turned[0])
        here = turned[j] if j < parts else jnp.zeros_like(turned[0])
        columns = pl.ds(start, LANES)
        tile_ref[s, c, rows, columns] = tile_ref[s, c, rows, columns] - jnp.where(lane < shift, above, here)


def planes(ref):
    return [(s, c) for s in range(ref.shape[0]) for c in range(ref.shape[1])]


AXIS = "lat"


def is_second():
    return lax.rem(lax.axis_index(AXIS), 2) == 1


def is_last():
    return lax.axis_index(AXIS) == lax.axis_size(AXIS) - 1


def larger(x0, x1):
    return jnp.where(x1 >= x0, 1, 0)


def ints_kernel(x_ref, y_ref, m_ref, out_ref):
    for i in range(2):
        out_ref[i] = x_ref[i]
        out_ref[2 + i] = y_ref[i]
        out_ref[4 + i] = m_ref[i]


def load_kernel(x_ref, y_ref, objects_ref, measured_ref, tile_ref, out_ref, sems):
    copies = []
    for k, (s, c) in enumerate(planes(tile_ref)):
        copies.append(pltpu.make_async_copy(objects_ref.at[s, c], tile_ref.at[s, c], sems.at[k]))
        copies[-1].start()
    b = larger(x_ref[0], x_ref[1])
    half, window = out_ref.shape[1:]
    picked = pltpu.make_async_copy(
        measured_ref.at[b], out_ref.at[pl.ds(len(copies), window // half)], sems.at[len(copies)])
    picked.start()
    for k, (s, c) in enumerate(planes(tile_ref)):
        copies[k].wait()
        parts = columns_at(tile_ref, s, c, pl.ds(tile_ref.shape[2] - half, half), y_ref[b], window)
        for j, part in enumerate(parts):
            out_ref[k, :, j * LANES : (j + 1) * LANES] = part
    picked.wait()


def put_rows(out_ref, index, tile_ref, s, c, start, y_offset):
    half, window = out_ref.shape[1:]
    rows = pl.ds(pl.multiple_of(start, 8), half)
    for j, part in enumerate(columns_at(tile_ref, s, c, rows, y_offset, window)):
        out_ref[index, :, j * LANES : (j + 1) * LANES] = part


def second_rows(left, half):
    b = larger(left[0], left[1])
    both = left[b] <= half
    return jnp.where(both, 0, half), jnp.where(both, left[2 + b], left[3 - b])


def pack_kernel(left, tile_ref, moved_ref, first_ref, pair_ref):
    half = first_ref.shape[1]
    y_first = left[3 - larger(left[0], left[1])]

    @pl.when(is_second())
    def _():
        start, y_second = second_rows(left, half)
        count = first_ref.shape[0]
        for k, (s, c) in enumerate(planes(tile_ref)):
            put_rows(pair_ref, k, tile_ref, s, c, 0, y_first)
            put_rows(pair_ref, count + k, tile_ref, s, c, start, y_second)

    @pl.when(jnp.logical_not(is_second()))
    def _():
        for k, (s, c) in enumerate(planes(tile_ref)):
            put_rows(first_ref, k, tile_ref, s, c, 0, y_first)
        pair_ref[0 : moved_ref.shape[0]] = moved_ref[...]


def pack_second_kernel(left, tile_ref, after_ref, out_ref):
    del after_ref

    @pl.when(jnp.logical_not(is_second()))
    def _():
        start, y_second = second_rows(left, out_ref.shape[1])
        for k, (s, c) in enumerate(planes(tile_ref)):
            put_rows(out_ref, k, tile_ref, s, c, start, y_second)


def call(kernel, name, args, specs, outs, scratch=(), aliases={}, flops=10**6, moved=2**21):
    return pl.pallas_call(
        kernel,
        in_specs=specs,
        out_specs=jax.tree.map(lambda _: VMEM, outs),
        out_shape=outs,
        scratch_shapes=scratch,
        input_output_aliases=aliases,
        compiler_params=PARAMS,
        cost_estimate=pl.CostEstimate(flops=flops, bytes_accessed=moved, transcendentals=0),
        name=name,
    )(*args)


def cmul(ar, ai, br, bi):
    return ar * br - ai * bi, ar * bi + ai * br


def cmul_conj(ar, ai, br, bi):
    return ar * br + ai * bi, ar * bi - ai * br


def window_kernel(slot, x_ref, y_ref, m_ref, left, tile_ref, *refs):
    if slot == 0:
        pair_ref, *refs = refs
    elif slot == 1:
        moved_ref, first_ref, *refs = refs
    else:
        pair_ref, first_ref, second_ref, *refs = refs
    probe_ref, measured_ref, high_ref, low_ref, *refs = refs
    refs = refs[(1, 3, 2)[slot] :]
    if slot < 2:
        total_ref, ret_ref, left_ret_ref, *refs = refs
    else:
        total_ref, ret_ref, *refs = refs
    extended, win, intensity, left_high, left_low, right_high, right_low, entry, field = refs
    slices, parts, tile, _ = tile_ref.shape
    count, half, window = ret_ref.shape[0] // 2, ret_ref.shape[1], ret_ref.shape[2]
    padded = window + 8

    b = larger(x_ref[0], x_ref[1])
    a = 1 - b
    keeps = jnp.logical_or(x_ref[b] <= half, is_last())
    left_b = larger(left[0], left[1])
    second = is_second()
    if slot < 2:
        incoming = second if slot == 0 else jnp.logical_not(second)
        left_moves = jnp.logical_and(left[left_b] > half, lax.axis_index(AXIS) > 0)
        here = jnp.logical_or(x_ref[a] <= half, is_last())
        active = jnp.logical_or(jnp.logical_and(incoming, left_moves),
                                jnp.logical_and(jnp.logical_not(incoming), here))
        mine = a
        x_offset = jnp.where(incoming, left[left_b] - half, x_ref[mine])
        y_offset = jnp.where(incoming, left[2 + left_b], y_ref[mine])
        mode = jnp.where(incoming, left[4 + left_b], m_ref[mine])
        tile_start = pl.multiple_of(jnp.where(incoming, half, 0), 8)
        other_start = pl.multiple_of(jnp.where(incoming, 0, tile), 8)
    else:
        active = jnp.logical_or(keeps, x_ref[a] > half)
        mine = jnp.where(keeps, b, a)
        x_offset, y_offset, mode = x_ref[mine], y_ref[mine], m_ref[mine]
        tile_start, other_start = 0, tile

    product = functools.partial(jnp.dot, preferred_element_type=jnp.float32)

    def transform(real, imag, table):
        left_high[:, 0:window], left_low[:, 0:window] = split(real)
        left_high[:, window:], left_low[:, window:] = split(imag)
        last = (product(left_high[...], high_ref[table]) + product(left_high[...], low_ref[table])
                + product(left_low[...], high_ref[table]))
        high, low = split(last[:, 0:window])
        right_high[0:window, 0:window] = high
        right_low[0:window, 0:window] = low
        right_high[window:, window:] = high
        right_low[window:, window:] = low
        high, low = split(last[:, window:])
        right_high[0:window, window:] = high
        right_low[0:window, window:] = low
        right_high[window:, 0:window] = -high
        right_low[window:, 0:window] = -low
        high, low = high_ref[table, 0:window], low_ref[table, 0:window]
        first = (product(high, right_high[...]) + product(high, right_low[...])
                 + product(low, right_high[...]))
        return first[:, 0:window], first[:, window:]

    def transform_conj(real, imag, table):
        real, imag = transform(real, -imag, table)
        return real, -imag

    @pl.when(active)
    def _():
        offset = lax.rem(x_offset, 8)
        base = pl.multiple_of(x_offset - offset, 8)

        def store_piece(s, piece):
            for c in range(parts):
                k = s * parts + c
                value = jnp.concatenate([piece[c], jnp.zeros((8, window), jnp.float32)], axis=0)
                extended[...] = jnp.zeros_like(extended)
                extended[pl.ds(base, padded), :] = pltpu.roll(value, offset, 0)
                subtract_at(total_ref, s, c, pl.ds(0, tile), y_offset, extended[pl.ds(tile_start, tile), :])
                if slot < 2:
                    @pl.when(incoming)
                    def _():
                        left_ret_ref[k] = extended[0:half]

                    @pl.when(jnp.logical_not(incoming))
                    def _():
                        ret_ref[k] = extended[tile : tile + half]
                else:
                    @pl.when(keeps)
                    def _():
                        ret_ref[count + k] = extended[tile : tile + half]

                    @pl.when(jnp.logical_not(keeps))
                    def _():
                        ret_ref[k] = extended[tile : tile + half]
                        ret_ref[count + k] = extended[tile + half : tile + 2 * half]

        for k, (s, c) in enumerate(planes(tile_ref)):
            rows = pl.ds(tile_start, tile)
            for j, part in enumerate(columns_at(tile_ref, s, c, pl.ds(0, tile), y_offset, window)):
                extended[rows, j * LANES : (j + 1) * LANES] = part
            if slot == 0:
                extended[pl.ds(other_start, half), :] = pair_ref[k]
                extended[tile + half : tile + 2 * half] = jnp.zeros((half, window), jnp.float32)
            elif slot == 1:
                extended[pl.ds(other_start, half), :] = jnp.where(incoming, moved_ref[k], first_ref[k])
                extended[tile + half : tile + 2 * half] = jnp.zeros((half, window), jnp.float32)
            else:
                one = jnp.where(second, first_ref[k], pair_ref[k])
                two = jnp.where(second, second_ref[k], pair_ref[count + k])
                extended[tile : tile + half] = jnp.where(keeps, two, one)
                extended[tile + half : tile + 2 * half] = jnp.where(keeps, 0.0, two)
            loaded = extended[pl.ds(base, padded), :]
            win[s, c] = pltpu.roll(loaded, padded - offset, 0)[:window]
        if slot < 2:
            source = pair_ref if slot == 0 else moved_ref

            @pl.when(incoming)
            def _():
                for k in range(window // half):
                    intensity[k * half : (k + 1) * half] = source[count + k]

            @pl.when(jnp.logical_not(incoming))
            def _():
                intensity[...] = measured_ref[mine]
        else:
            intensity[...] = measured_ref[mine]

        entry[0], entry[1] = transform(*cmul(probe_ref[mode, 0], probe_ref[mode, 1], win[0, 0], win[0, 1]), 0)
        fr, fi = transform(*cmul(entry[0], entry[1], win[1, 0], win[1, 1]), 1)
        residual = fr * fr + fi * fi - intensity[...]
        field[0], field[1] = transform_conj(residual * fr, residual * fi, 1)
        store_piece(1, cmul_conj(entry[0], entry[1], field[0], field[1]))
        field[0], field[1] = transform_conj(*cmul_conj(win[1, 0], win[1, 1], field[0], field[1]), 0)
        store_piece(0, cmul_conj(probe_ref[mode, 0], probe_ref[mode, 1], field[0], field[1]))


def moved_kernel(x_ref, y_ref, piece_ref, state_ref, out_ref):
    del state_ref
    half = piece_ref.shape[1]
    b = larger(x_ref[0], x_ref[1])

    @pl.when(jnp.logical_and(x_ref[b] > half, jnp.logical_not(is_last())))
    def _():
        for k, (s, c) in enumerate(planes(out_ref)):
            subtract_at(out_ref, s, c, pl.ds(out_ref.shape[2] - half, half), y_ref[b], piece_ref[k])


def final_kernel(left, piece_ref, state_ref, out_ref, total_ref, sems):
    del state_ref
    half = piece_ref.shape[1]
    b = larger(left[0], left[1])
    start, y_second = second_rows(left, half)
    start = pl.multiple_of(start, 8)
    used = jnp.logical_or(left[b] <= half, left[1 - b] > half)
    copies = []
    for k, (s, c) in enumerate(planes(total_ref)):
        subtract_at(total_ref, s, c, pl.ds(0, half), left[3 - b], piece_ref[k])

        @pl.when(used)
        def _():
            subtract_at(total_ref, s, c, pl.ds(start, half), y_second, piece_ref[piece_ref.shape[0] // 2 + k])

        copies.append(pltpu.make_async_copy(total_ref.at[s, c], out_ref.at[s, c], sems.at[k]))
        copies[-1].start()
    for copy in copies:
        copy.wait()


def on_device(objects, probes, x_offsets, y_offsets, modes, measured):
    window = measured.shape[-1]
    slices, parts, tile, _ = objects.shape
    count, half = slices * parts, tile // 2
    tables = [on_chip(t) for t in matrix_tables(window)]
    total, probes = on_chip(objects), on_chip(probes)
    rows = lambda n: pltpu.VMEM((n, half, window), jnp.float32)
    shape = pltpu.VMEM(objects.shape, jnp.float32)
    odd, even = (lambda i: i % 2 == 1), (lambda i: i % 2 == 0)
    left_across, right_across = route(AXIS, -1, even), route(AXIS, 1, odd)
    within = route(AXIS, -1, odd) + route(AXIS, 1, even)

    ints = pl.pallas_call(
        ints_kernel,
        in_specs=[SMEM] * 3,
        out_specs=SMEM,
        out_shape=jax.ShapeDtypeStruct((6,), jnp.int32),
        name="ints",
    )(x_offsets, y_offsets, modes)
    left = permute_pairs(ints, AXIS, route(AXIS, 1))
    any_space = pl.BlockSpec(memory_space=pl.ANY)
    tile_here, moved = call(
        load_kernel, "load", (x_offsets, y_offsets, objects, measured.reshape(-1, window // half, half, window)),
        [SMEM, SMEM, any_space, any_space], [shape, rows(count + window // half)],
        [pltpu.SemaphoreType.DMA((count + 1,))])
    moved_in = on_chip(permute_pairs(moved, AXIS, right_across))
    first, pair = call(
        pack_kernel, "pack", (left, tile_here, moved), [SMEM, VMEM, VMEM], [rows(count), rows(2 * count)])
    first_in = on_chip(permute_pairs(first, AXIS, left_across))
    pair_in = on_chip(permute_pairs(pair, AXIS, within))

    scratch = [
        pltpu.VMEM((tile + window + 8, window), jnp.float32),
        pltpu.VMEM((slices, parts, window, window), jnp.float32),
        pltpu.VMEM((window, window), jnp.float32),
        *[pltpu.VMEM((window, 2 * window), jnp.bfloat16)] * 2,
        *[pltpu.VMEM((2 * window, 2 * window), jnp.bfloat16)] * 2,
        pltpu.VMEM((parts, window, window), jnp.float32),
        pltpu.VMEM((parts, window, window), jnp.float32),
    ]
    measured = on_chip(measured)

    def slot(index, data, carried, outs):
        args = (x_offsets, y_offsets, modes, left, tile_here, *data, probes, measured, *tables, *carried)
        first_carried = len(args) - len(carried)
        return call(
            functools.partial(window_kernel, index), "slot" + str(index), args,
            [SMEM] * 4 + [VMEM] * (len(args) - 4), outs, scratch,
            {first_carried + k: k for k in range(len(carried))}, 5 * 10**9, 6 * 2**20)

    total, ret, left_ret = slot(0, (pair_in,), (total,), [shape, rows(2 * count), rows(count)])
    second = call(
        pack_second_kernel, "pack_second", (left, tile_here, left_ret),
        [SMEM, VMEM, any_space], rows(count))
    second_in = on_chip(permute_pairs(second, AXIS, left_across))
    total, ret, left_ret = slot(
        1, (moved_in, first_in), (total, ret, left_ret), [shape, rows(2 * count), rows(count)])
    moved_back = on_chip(permute_pairs(left_ret, AXIS, route(AXIS, -1)))
    total, ret = slot(2, (pair_in, first_in, second_in), (total, ret), [shape, rows(2 * count)])
    returned = on_chip(permute_pairs(ret, AXIS, route(AXIS, 1)))
    total = call(
        moved_kernel, "moved", (x_offsets, y_offsets, moved_back, total),
        [SMEM, SMEM, VMEM, VMEM], shape, aliases={3: 0})
    return pl.pallas_call(
        final_kernel,
        in_specs=[SMEM, VMEM, VMEM],
        out_specs=[any_space, VMEM],
        out_shape=[jax.ShapeDtypeStruct(objects.shape, jnp.float32), shape],
        scratch_shapes=[pltpu.SemaphoreType.DMA((count,))],
        input_output_aliases={2: 1},
        compiler_params=PARAMS,
        name="final",
    )(left, returned, total)[0]


def solution(mesh):
    in_specs = (
        P(None, None, ("groups", "lat"), None),
        P("groups", None, None, None),
        P(("groups", "lat")),
        P(("groups", "lat")),
        P(("groups", "lat")),
        P(("groups", "lat"), None, None),
    )
    out_specs = P(None, None, ("groups", "lat"), None)
    return jax.shard_map(
        on_device, mesh=mesh, in_specs=in_specs, out_specs=out_specs, check_vma=False
    )
```
